32 devices in a mesh: seq: 8 (over y, x, core), tensor: 4 (over z).
Axes of the slice: x: 2, y: 2, z: 4, core: 2. Of those that a mesh axis runs over, the one named last changes fastest.
Arguments:
- queries: bfloat16 [1024, 4096], P(('seq', 'tensor')), may hold values from -5 to 5
- keys: bfloat16 [1024, 1024], P(('seq', 'tensor')), may hold values from -5 to 5
- values: bfloat16 [1024, 1024], P(('seq', 'tensor')), may hold values from -5 to 5
- mamba_x: bfloat16 [1024, 8192], P(('seq', 'tensor')), may hold values from -5 to 5
- mamba_b: bfloat16 [1024, 1024], P(('seq', 'tensor')), may hold values from -5 to 5
- mamba_c: bfloat16 [1024, 1024], P(('seq', 'tensor')), may hold values from -5 to 5
- mamba_dt: bfloat16 [1024, 128], P(('seq', 'tensor')), may hold values from -4 to 4
- conv_x: bfloat16 [4, 8192], P(None, 'tensor'), may hold values from -3 to 3
- conv_b: bfloat16 [4, 1024], P(None, 'tensor'), may hold values from -3 to 3
- conv_c: bfloat16 [4, 1024], P(None, 'tensor'), may hold values from -3 to 3
- dt_bias: float32 [128], P('tensor'), may hold values from -1 to 1
- decay_rate: float32 [128], P('tensor'), may hold values from 0.0001 to 0.05
- skip_gain: float32 [128], P('tensor'), may hold values from 0.5 to 1.5
- norm_gain: float32 [8192], P('tensor'), may hold values from 0.5 to 1.5
- windows: int32 [32], replicated, may hold values from 160 to 640, as said below
- doc_lengths: int32 [3], replicated, may hold values from 1 to 768, 1024 in all
Outputs:
- attn_out: bfloat16 [1024, 4096], P('seq', 'tensor')
- mamba_out: bfloat16 [1024, 8192], P('seq', 'tensor')
- attn_checksum: float32 [4096], P('tensor')
- mamba_checksum: float32 [8192], P('tensor')
The draws below stay inside these ranges and needn't reach their ends.
Inputs may be any that keep to these rules, and one draw needn't show every extreme that they name: `windows`: one of the 32 query heads has a window of exactly 640 tokens. `doc_lengths`: 3 lengths summing to 1024; the longest is exactly three quarters of 1024.
All inputs are finite; a program needn't handle non-finite values.
Results may differ from the reference program's by a relative error of at most 0.007.
Values may be sent and summed in bfloat16 or wider, within the bound.
No kernel may reach another device: no remote copies, remote signals or barrier semaphores. Data moves between devices by JAX's collectives and lax.ppermute only.
A program may use at most 192 MiB of HBM per device.

```python
import math
import jax
import jax.numpy as jnp
import numpy as np
from jax import lax

QUERY_HEAD_COUNT = 32
KEY_VALUE_HEADS = 8
HEAD_SIZE = 128
MH = 128
MP = 64
MN = 128
MG = 8
KC = 4
NDOC = 3
TOKENS_PER_INDEX = 128
SEQUENCE_LENGTH = 1024
LONGEST_WINDOW = 640


def keys_common(key):
    starting_key = jax.random.fold_in(key, 101)
    unscaled_keys = jnp.clip(jax.random.normal(starting_key, (SEQUENCE_LENGTH, KEY_VALUE_HEADS * HEAD_SIZE), jnp.float32), -5.0, 5.0)
    return unscaled_keys


def draw_keys(key, part):
    return keys_common(key).astype(jnp.bfloat16)


def draw_queries(key, part):
    drawn_rows = jnp.clip(jax.random.normal(jax.random.fold_in(key, 202), (SEQUENCE_LENGTH, QUERY_HEAD_COUNT * HEAD_SIZE), jnp.float32), -5.0, 5.0)
    return drawn_rows.astype(jnp.bfloat16)


def draw_windows(key, part):
    widths = jax.random.randint(jax.random.fold_in(key, 303), (QUERY_HEAD_COUNT,), LONGEST_WINDOW // 4, LONGEST_WINDOW + 1)
    chosen = jax.random.randint(jax.random.fold_in(key, 304), (), 0, QUERY_HEAD_COUNT)
    return jnp.where(jnp.arange(QUERY_HEAD_COUNT) == chosen, LONGEST_WINDOW, widths).astype(jnp.int32)


def block_levels(own_key, shape, split, least, top_value):
    loudness = 1.0
    for axis_at, shards_of in split:
        steps = jax.random.uniform(jax.random.fold_in(jax.random.fold_in(own_key, 6), axis_at), (shards_of,), jnp.float32, least / len(split), top_value / len(split))
        loudness = loudness * jnp.repeat(jnp.exp(steps), shape[axis_at] // shards_of).reshape((-1,) + (1,) * (len(shape) - 1 - axis_at))
    return loudness


def profile(number_of, total, most, lean):
    loads = [(1 << 20) // math.isqrt(grade ** lean) + 1 for grade in range(2, number_of + 1)]
    spare, counts = total - most - (number_of - 1), [1] * (number_of - 1)
    while spare > 0:
        movable = [i for i in range(number_of - 1) if counts[i] < most]
        mass, left = sum([loads[i] for i in movable]), spare
        for i in movable:
            more = min(most - counts[i], max(1, left * loads[i] // mass), spare)
            counts[i] = counts[i] + more
            spare = spare - more
    return np.array([most] + counts)


def ragged_sizes(key, amount, total, most, skew):
    if amount == 2:
        one = jax.random.randint(key, (), max(1, total - most), min(most, total - 1) + 1)
        return jnp.stack([one, total - one])
    lengths = jnp.asarray(profile(amount, total, most, skew), jnp.int32)
    couples = (amount - 1) // 2
    giver, taker = lengths[1:1 + 2 * couples:2], lengths[2:2 + 2 * couples:2]
    slack = jnp.minimum(giver - 1, most - taker)
    shifted = jax.random.randint(jax.random.fold_in(key, 1), (couples,), 0, 1 << 20) % (slack + 1)
    lengths = lengths.at[1:1 + 2 * couples:2].set(giver - shifted).at[2:2 + 2 * couples:2].set(taker + shifted)
    return lengths[jax.random.permutation(jax.random.fold_in(key, 2), amount)]


def noise(own_key, shape, width, reach, cuts=(), kind=jnp.bfloat16):
    loudness = block_levels(own_key, shape, cuts, -0.22, 0.18) if cuts else 1.0
    result = jax.random.normal(own_key, shape, jnp.float32) * width * loudness
    return jnp.minimum(jnp.maximum(result, -reach), reach).astype(kind)


def setup_inputs(seed: int = 0) -> dict:
    splits = jax.random.split(jax.random.key(seed), 17)
    return {
        "queries": draw_queries(jax.random.fold_in(splits[16], 71), 0),
        "keys": draw_keys(jax.random.fold_in(splits[16], 71), 0),
        "values": noise(splits[2], (SEQUENCE_LENGTH, KEY_VALUE_HEADS * HEAD_SIZE), 1.0, 5.0, ((0, 32),)),
        "mamba_x": noise(splits[3], (SEQUENCE_LENGTH, MH * MP), 1.0, 5.0, ((0, 32),)),
        "mamba_b": noise(splits[4], (SEQUENCE_LENGTH, MG * MN), 1.0, 5.0, ((0, 32),)),
        "mamba_c": noise(splits[5], (SEQUENCE_LENGTH, MG * MN), 1.0, 5.0, ((0, 32),)),
        "mamba_dt": noise(splits[6], (SEQUENCE_LENGTH, MH), 1.0, 4.0, ((0, 32),)),
        "conv_x": noise(splits[7], (KC, MH * MP), KC ** -0.5, 3.0, ((1, 4),)),
        "conv_b": noise(splits[8], (KC, MG * MN), KC ** -0.5, 3.0, ((1, 4),)),
        "conv_c": noise(splits[9], (KC, MG * MN), KC ** -0.5, 3.0, ((1, 4),)),
        "dt_bias": jnp.clip(jax.random.uniform(splits[10], (MH,), jnp.float32, -1.0, 1.0) * block_levels(splits[10], (MH,), ((0, 4),), -0.4, 0.0), -1.0, 1.0),
        "decay_rate": jnp.clip(jnp.exp(math.log(0.05) - 6.214608 * jax.random.uniform(splits[11], (MH,), jnp.float32) ** block_levels(splits[11], (MH,), ((0, 4),), -0.2, 0.2)), 0.0001, 0.05),
        "skip_gain": jnp.clip(0.5 + 1.0 * jax.random.uniform(splits[12], (MH,), jnp.float32) ** block_levels(splits[12], (MH,), ((0, 4),), -0.2, 0.2), 0.5, 1.5),
        "norm_gain": jnp.clip(1.0 + 0.1 * jax.random.normal(splits[13], (MH * MP,), jnp.float32), 0.5, 1.5),
        "windows": draw_windows(jax.random.fold_in(splits[16], 71), 0),
        "doc_lengths": ragged_sizes(splits[15], NDOC, SEQUENCE_LENGTH, 3 * SEQUENCE_LENGTH // 4, 1).astype(jnp.int32),
    }


NEG_LARGE = -1e+30
EPS_NORM = 1e-05

def doc_table(doc_lengths):
    return (jnp.cumsum(doc_lengths) - doc_lengths).astype(jnp.int32)

def doc_index(positions, doc_starts):
    return lax.optimization_barrier(jnp.sum((positions[:, None] >= doc_starts[None, :]).astype(jnp.int32), axis=1)) - 1

def allowed_mask(query_pos, key_pos, doc_starts, window_per_head):
    gap = query_pos[:, None] - key_pos[None, :]
    same_doc = doc_index(query_pos, doc_starts)[:, None] == doc_index(key_pos, doc_starts)[None, :]
    base_ok = (gap >= 0) & (key_pos[None, :] >= 0) & same_doc
    return base_ok[None, None] & (gap[None, None] < window_per_head[:, :, None, None])

def reference_attention(queries, keys, values, windows, doc_starts):
    group_width = QUERY_HEAD_COUNT // KEY_VALUE_HEADS
    window_per_head = windows.reshape(KEY_VALUE_HEADS, group_width)
    block_count = SEQUENCE_LENGTH // TOKENS_PER_INDEX
    padded_keys = jnp.pad(keys, ((LONGEST_WINDOW, 0), (0, 0)))
    padded_values = jnp.pad(values, ((LONGEST_WINDOW, 0), (0, 0)))

    def one_block(index):
        first = (index * TOKENS_PER_INDEX).astype(jnp.int32)
        query_tile_block = lax.dynamic_slice_in_dim(queries, first, TOKENS_PER_INDEX, 0)
        key_tile_block = lax.dynamic_slice_in_dim(padded_keys, first, LONGEST_WINDOW + TOKENS_PER_INDEX, 0)
        value_tile_block = lax.dynamic_slice_in_dim(padded_values, first, LONGEST_WINDOW + TOKENS_PER_INDEX, 0)
        query_pos = first + jnp.arange(TOKENS_PER_INDEX, dtype=jnp.int32)
        key_pos = first - LONGEST_WINDOW + jnp.arange(LONGEST_WINDOW + TOKENS_PER_INDEX, dtype=jnp.int32)
        grouped_heads = query_tile_block.reshape(TOKENS_PER_INDEX, KEY_VALUE_HEADS, group_width, HEAD_SIZE).astype(jnp.float32)
        keys_rank3 = key_tile_block.reshape(LONGEST_WINDOW + TOKENS_PER_INDEX, KEY_VALUE_HEADS, HEAD_SIZE).astype(jnp.float32)
        values_rank3 = value_tile_block.reshape(LONGEST_WINDOW + TOKENS_PER_INDEX, KEY_VALUE_HEADS, HEAD_SIZE).astype(jnp.float32)
        scores = jnp.einsum('tgqd,sgd->gqts', grouped_heads, keys_rank3) * (1.0 / math.sqrt(HEAD_SIZE))
        allowed = allowed_mask(query_pos, key_pos, doc_starts, window_per_head)
        scores = jnp.where(allowed, scores, NEG_LARGE)
        top_score = lax.optimization_barrier(jnp.max(scores, axis=-1, keepdims=True))
        weights = jnp.where(allowed, jnp.exp(scores - top_score), 0.0)
        totals = lax.optimization_barrier(jnp.sum(weights, axis=-1))
        rounded = weights.astype(jnp.bfloat16).astype(jnp.float32)
        mixed = jnp.einsum('gqts,sgd->gqtd', rounded, values_rank3)
        output = mixed / totals[..., None]
        return output.transpose(2, 0, 1, 3).reshape(TOKENS_PER_INDEX, QUERY_HEAD_COUNT * HEAD_SIZE).astype(jnp.bfloat16)
    blocks = lax.map(one_block, jnp.arange(block_count, dtype=jnp.int32))
    return blocks.reshape(SEQUENCE_LENGTH, QUERY_HEAD_COUNT * HEAD_SIZE)

def causal_conv(extended, taps, positions, doc_starts):
    count = positions.shape[0]
    docs_out = doc_index(positions, doc_starts)
    ext_pos = positions[0] - (KC - 1) + jnp.arange(count + KC - 1, dtype=jnp.int32)
    docs_ext = doc_index(ext_pos, doc_starts)
    running = jnp.zeros((count, extended.shape[1]), jnp.float32)
    for tap_index in range(KC):
        offset = KC - 1 - tap_index
        valid = (docs_ext[offset:offset + count] == docs_out) & (ext_pos[offset:offset + count] >= 0)
        term = taps[tap_index].astype(jnp.float32)[None, :] * extended[offset:offset + count].astype(jnp.float32)
        running = running + jnp.where(valid[:, None], term, 0.0)
    return jax.nn.silu(running).astype(jnp.bfloat16)

def stretch_terms(x_rows, b_rows, c_rows, dt_rows, positions, doc_starts, dt_bias, decay_rate):
    count = positions.shape[0]
    heads = x_rows.shape[1] // MP
    groups = b_rows.shape[1] // MN
    per_group = heads // groups
    docs = doc_index(positions, doc_starts)
    prior_doc = doc_index(positions[:1] - 1, doc_starts)[0]
    delta = jax.nn.softplus(dt_rows.astype(jnp.float32) + dt_bias[None, :])
    log_decay = -delta * decay_rate[None, :]
    running = jnp.cumsum(log_decay, axis=0)
    running_heads = running.T
    order = jnp.arange(count, dtype=jnp.int32)
    causal = order[:, None] >= order[None, :]
    same_doc = docs[:, None] == docs[None, :]
    gaps = running_heads[:, :, None] - running_heads[:, None, :]
    segment = jnp.where((causal & same_doc)[None], jnp.exp(jnp.minimum(gaps, 0.0)), 0.0)
    inputs3 = x_rows.reshape(count, heads, MP)
    b_groups = b_rows.reshape(count, groups, MN)
    c_groups = c_rows.reshape(count, groups, MN)
    cross = jnp.einsum('tgn,sgn->gts', c_groups.astype(jnp.float32), b_groups.astype(jnp.float32))
    cross_heads = jnp.repeat(cross, per_group, axis=0)
    mixing = (segment * cross_heads * delta.T[:, None, :]).astype(jnp.bfloat16)
    intra = jnp.einsum('hts,shp->thp', mixing.astype(jnp.float32), inputs3.astype(jnp.float32))
    last_doc = docs[count - 1]
    to_end = jnp.where((docs == last_doc)[:, None], jnp.exp(running[count - 1][None, :] - running), 0.0) * delta
    weighted = (inputs3.astype(jnp.float32) * to_end[:, :, None]).astype(jnp.bfloat16)
    b_heads = jnp.repeat(b_groups, per_group, axis=1)
    local_state = jnp.einsum('shp,shn->hpn', weighted.astype(jnp.float32), b_heads.astype(jnp.float32))
    carry_factor = jnp.where(prior_doc == last_doc, jnp.exp(running[count - 1]), 0.0)
    inflow = jnp.where((docs == prior_doc)[:, None], jnp.exp(running), 0.0)
    c_heads = jnp.repeat(c_groups, per_group, axis=1)
    return (intra, local_state, carry_factor, inflow, c_heads)

def stretch_finish(intra, incoming, inflow, c_heads, x_rows, skip_gain, norm_gain):
    count = x_rows.shape[0]
    heads = x_rows.shape[1] // MP
    incoming_bf = incoming.astype(jnp.bfloat16)
    entering = jnp.einsum('thn,hpn->thp', c_heads.astype(jnp.float32), incoming_bf.astype(jnp.float32)) * inflow[:, :, None]
    inputs3 = x_rows.reshape(count, heads, MP).astype(jnp.float32)
    mixed = intra + entering + skip_gain[None, :, None] * inputs3
    mean_square = lax.optimization_barrier(jnp.mean(mixed * mixed, axis=-1, keepdims=True))
    normed = mixed * lax.rsqrt(mean_square + EPS_NORM) * norm_gain.reshape(heads, MP)[None]
    return normed.reshape(count, heads * MP).astype(jnp.bfloat16)

def reference(queries, keys, values, mamba_x, mamba_b, mamba_c, mamba_dt, conv_x, conv_b, conv_c, dt_bias, decay_rate, skip_gain, norm_gain, windows, doc_lengths):
    doc_starts = doc_table(doc_lengths)
    attention = reference_attention(queries, keys, values, windows, doc_starts)
    positions = jnp.arange(SEQUENCE_LENGTH, dtype=jnp.int32)
    pad_rows = ((KC - 1, 0), (0, 0))
    conv_x_out = causal_conv(jnp.pad(mamba_x, pad_rows), conv_x, positions, doc_starts)
    conv_b_out = causal_conv(jnp.pad(mamba_b, pad_rows), conv_b, positions, doc_starts)
    conv_c_out = causal_conv(jnp.pad(mamba_c, pad_rows), conv_c, positions, doc_starts)
    stretch_count = SEQUENCE_LENGTH // TOKENS_PER_INDEX

    def stretch_step(incoming, inputs):
        index, x_rows, b_rows, c_rows, dt_rows = inputs
        stretch_pos = index * TOKENS_PER_INDEX + jnp.arange(TOKENS_PER_INDEX, dtype=jnp.int32)
        intra, local_state, carry_factor, inflow, c_heads = stretch_terms(x_rows, b_rows, c_rows, dt_rows, stretch_pos, doc_starts, dt_bias, decay_rate)
        output = stretch_finish(intra, incoming, inflow, c_heads, x_rows, skip_gain, norm_gain)
        updated = carry_factor[:, None, None] * incoming + local_state
        return (updated, output)
    initial = jnp.zeros((MH, MP, MN), jnp.float32)
    scanned = (jnp.arange(stretch_count, dtype=jnp.int32), conv_x_out.reshape(stretch_count, TOKENS_PER_INDEX, MH * MP), conv_b_out.reshape(stretch_count, TOKENS_PER_INDEX, MG * MN), conv_c_out.reshape(stretch_count, TOKENS_PER_INDEX, MG * MN), mamba_dt.reshape(stretch_count, TOKENS_PER_INDEX, MH))
    final_state, outputs = lax.scan(stretch_step, initial, scanned)
    mamba_out = outputs.reshape(SEQUENCE_LENGTH, MH * MP)
    return (attention, mamba_out, lax.optimization_barrier(jnp.sum(attention.astype(jnp.float32), axis=0)), lax.optimization_barrier(jnp.sum(mamba_out.astype(jnp.float32), axis=0)))
```

```python
import functools
import math

import jax
import jax.numpy as jnp
from jax import lax
from jax.experimental import pallas as pl
from jax.experimental.pallas import tpu as pltpu
from jax.sharding import Mesh, PartitionSpec as P

HEAD_SIZE = 128
MP = 64
MN = 128
KC = 4
HALO = 8
NEG_LARGE = -1e30
EPS_NORM = 1e-05
PAIR = 2

F32 = jnp.float32
BF16 = jnp.bfloat16


def doc_count(pos, lengths_ref):
    start = jnp.int32(0)
    count = jnp.zeros(pos.shape, jnp.int32) if not isinstance(pos, int) else jnp.int32(0)
    for k in range(lengths_ref.shape[0]):
        count = count + jnp.where(pos >= start, 1, 0)
        start = start + lengths_ref[k]
    return count


def doc_scalar(pos, lengths_ref):
    start = jnp.int32(0)
    count = jnp.int32(0)
    for k in range(lengths_ref.shape[0]):
        count = count + (pos >= start).astype(jnp.int32)
        start = start + lengths_ref[k]
    return count


def softplus(x):
    return jnp.maximum(x, 0.0) + jnp.log1p(jnp.exp(-jnp.abs(x)))


def pair_lanes(first, second, rows):
    lane = lax.broadcasted_iota(jnp.int32, (rows, 2 * MP), 1)
    return jnp.where(lane < MP, first, second)


def pre_kernel(ids, lengths, rows_ref, halo_ref, taps_ref, prow_ref, conv_ref, pay_ref, cum_ref, ext):
    tokens = rows_ref.shape[0]
    width = taps_ref.shape[1]
    heads = prow_ref.shape[1]
    xw = width - 2 * MN
    first = ids[0] * tokens
    pos = first + lax.broadcasted_iota(jnp.int32, (tokens, 1), 0)
    here = doc_count(pos, lengths)
    same = [(doc_count(pos - j, lengths) == here).astype(F32) for j in range(1, KC)]
    step = 2 * MP
    for c in range(0, width, step):
        ext[0:HALO, :] = halo_ref[:, c : c + step].astype(F32)
        ext[HALO : HALO + tokens, :] = rows_ref[:, c : c + step].astype(F32)
        taps = taps_ref[:, c : c + step].astype(F32)
        u = taps[0:1, :] * ext[HALO : HALO + tokens, :]
        for j in range(1, KC):
            u = u + (taps[j : j + 1, :] * ext[HALO - j : HALO - j + tokens, :]) * same[j - 1]
        conv_ref[:, c : c + step] = (u / (1.0 + jnp.exp(-u))).astype(BF16)
    delta = softplus(rows_ref[:, width : width + heads].astype(F32) + prow_ref[0:1, :])
    logd = -delta * prow_ref[1:2, :]
    r = lax.broadcasted_iota(jnp.int32, (tokens, tokens), 0)
    s = lax.broadcasted_iota(jnp.int32, (tokens, tokens), 1)
    cum = jnp.dot(
        (r >= s).astype(F32), logd, precision=lax.Precision.HIGHEST, preferred_element_type=F32
    )
    cum_ref[...] = cum
    last_doc = doc_scalar(first + tokens - 1, lengths)
    to_end = jnp.where(here == last_doc, jnp.exp(cum[tokens - 1 : tokens, :] - cum), 0.0) * delta
    bc = conv_ref[:, xw : xw + MN]
    for k in range(heads // 2):
        weighted = (
            conv_ref[:, k * step : (k + 1) * step].astype(F32)
            * pair_lanes(to_end[:, 2 * k : 2 * k + 1], to_end[:, 2 * k + 1 : 2 * k + 2], tokens)
        ).astype(BF16)
        state = lax.dot_general(
            weighted, bc, (((0,), (0,)), ((), ())), preferred_element_type=F32
        )
        pay_ref[k * step : (k + 1) * step, :] = state.astype(BF16)
    ones = jnp.ones((tokens, MN), F32)
    total = lax.dot_general(
        logd, ones, (((0,), (0,)), ((), ())), precision=lax.Precision.HIGHEST,
        preferred_element_type=F32,
    )
    high = total.astype(BF16)
    pay_ref[xw : xw + heads, :] = high
    pay_ref[xw + heads : xw + 2 * heads, :] = (total - high.astype(F32)).astype(BF16)


def intra_kernel(ids, lengths, rows_ref, conv_ref, cum_ref, prow_ref, pcol_ref, out_ref):
    tokens = rows_ref.shape[0]
    heads = prow_ref.shape[1]
    xw = heads * MP
    half = tokens // PAIR
    step = 2 * MP
    dt = rows_ref[:, xw + 2 * MN : xw + 2 * MN + heads]
    eye = (
        lax.broadcasted_iota(jnp.int32, (heads, heads), 0)
        == lax.broadcasted_iota(jnp.int32, (heads, heads), 1)
    ).astype(BF16)
    dt_t = lax.dot_general(eye, dt, (((1,), (1,)), ((), ())), preferred_element_type=F32)
    delta_t = softplus(dt_t + pcol_ref[:, 0:1])
    logd_t = -delta_t * pcol_ref[:, 1:2]
    r = lax.broadcasted_iota(jnp.int32, (tokens, tokens), 0)
    s = lax.broadcasted_iota(jnp.int32, (tokens, tokens), 1)
    cum_t = jnp.dot(
        logd_t, (r <= s).astype(F32), precision=lax.Precision.HIGHEST, preferred_element_type=F32
    )
    first = ids[0] * tokens
    for b in range(PAIR):
        top, end = b * half, (b + 1) * half
        rpos = first + top + lax.broadcasted_iota(jnp.int32, (half, 1), 0)
        cpos = first + lax.broadcasted_iota(jnp.int32, (1, end), 1)
        allowed = (rpos >= cpos) & (doc_count(rpos, lengths) == doc_count(cpos, lengths))
        cross = lax.dot_general(
            conv_ref[top:end, xw + MN : xw + 2 * MN],
            conv_ref[0:end, xw : xw + MN],
            (((1,), (1,)), ((), ())),
            preferred_element_type=F32,
        )
        cross = jnp.where(allowed, cross, 0.0)
        lane = lax.broadcasted_iota(jnp.int32, (half, step), 1)
        for k in range(heads // 2):
            inputs = conv_ref[0:end, k * step : (k + 1) * step]
            parts = []
            for h in (2 * k, 2 * k + 1):
                gaps = cum_ref[top:end, h : h + 1] - cum_t[h : h + 1, 0:end]
                mix = cross * jnp.exp(jnp.minimum(gaps, 0.0)) * delta_t[h : h + 1, 0:end]
                parts.append(jnp.dot(mix.astype(BF16), inputs, preferred_element_type=F32))
            skip = jnp.where(
                lane < MP, prow_ref[2:3, 2 * k : 2 * k + 1], prow_ref[2:3, 2 * k + 1 : 2 * k + 2]
            )
            own = conv_ref[top:end, k * step : (k + 1) * step].astype(F32)
            out_ref[top:end, k * step : (k + 1) * step] = (
                jnp.where(lane < MP, parts[0], parts[1]) + skip * own
            )


def finish_kernel(count, ids, lengths, *refs):
    pays = refs[:count]
    intra_ref, conv_ref, cum_ref, gain_ref, own_ref, other_ref, sum_ref, full = refs[count:]
    tokens = intra_ref.shape[0]
    heads = cum_ref.shape[1]
    xw = heads * MP
    step = 2 * MP
    half = tokens // PAIR
    first = ids[0] * tokens
    incoming = jnp.zeros((heads, MP, MN), F32)
    total = jnp.zeros((heads, MN), F32)
    prior_doc = doc_scalar(first - 1, lengths)
    for d in range(1, count + 1):
        pay = pays[d - 1]
        reached = (doc_scalar(first - (d - 1) * tokens - 1, lengths) == prior_doc).astype(F32)
        weight = jnp.exp(total) * reached
        incoming = incoming + pay[0:xw, :].astype(F32).reshape(heads, MP, MN) * weight[:, None, :]
        total = (
            total
            + pay[xw : xw + heads, :].astype(F32)
            + pay[xw + heads : xw + 2 * heads, :].astype(F32)
        )
    state = incoming.reshape(xw, MN).astype(BF16)
    pos = first + lax.broadcasted_iota(jnp.int32, (tokens, 1), 0)
    inflow = jnp.where(doc_count(pos, lengths) == prior_doc, jnp.exp(cum_ref[...]), 0.0)
    cc = conv_ref[:, xw + MN : xw + 2 * MN]
    same_head = (
        lax.broadcasted_iota(jnp.int32, (step, step), 0) // MP
        == lax.broadcasted_iota(jnp.int32, (step, step), 1) // MP
    )
    mean = jnp.where(same_head, 1.0 / MP, 0.0).astype(BF16)
    for k in range(heads // 2):
        cols = slice(k * step, (k + 1) * step)
        entering = lax.dot_general(
            cc, state[cols, :], (((1,), (1,)), ((), ())), preferred_element_type=F32
        )
        mixed = intra_ref[:, cols] + entering * pair_lanes(
            inflow[:, 2 * k : 2 * k + 1], inflow[:, 2 * k + 1 : 2 * k + 2], tokens
        )
        square = mixed * mixed
        high = square.astype(BF16)
        low = (square - high.astype(F32)).astype(BF16)
        mean_square = jnp.dot(high, mean, preferred_element_type=F32) + jnp.dot(
            low, mean, preferred_element_type=F32
        )
        normed = (mixed * lax.rsqrt(mean_square + EPS_NORM) * gain_ref[0:1, cols]).astype(BF16)
        sum_ref[:, cols] = jnp.sum(normed.astype(F32), axis=0, keepdims=True)
        full[:, cols] = normed
    split_tokens(ids, full, own_ref, other_ref, half)


def split_tokens(ids, full, own_ref, other_ref, half):
    @pl.when(ids[1] == 0)
    def _():
        own_ref[...] = full[0:half, :]
        other_ref[...] = full[half:, :]

    @pl.when(ids[1] != 0)
    def _():
        own_ref[...] = full[half:, :]
        other_ref[...] = full[0:half, :]


def attention_kernel(ids, lengths, windows, rows_ref, kv_ref, own_ref, other_ref, sum_ref, full, top, den, acc):
    tokens = rows_ref.shape[0]
    shared = kv_ref.shape[2] // (2 * HEAD_SIZE)
    heads = full.shape[1] // HEAD_SIZE
    per = heads // shared
    half = tokens // PAIR
    qw = heads * HEAD_SIZE
    first = ids[0] * tokens
    base = ids[2]
    widest = windows[base]
    for h in range(1, heads):
        widest = jnp.maximum(widest, windows[base + h])
    qpos = first + lax.broadcasted_iota(jnp.int32, (tokens, 1), 0)
    qdoc = doc_count(qpos, lengths)
    ones = jnp.ones((tokens, HEAD_SIZE), BF16)
    scale = 1.0 / math.sqrt(HEAD_SIZE)

    def piece(d, keys, values, start):
        kpos = (first - d * tokens) + lax.broadcasted_iota(jnp.int32, (1, tokens), 1)
        gap = qpos - kpos
        ok = (gap >= 0) & (kpos >= 0) & (qdoc == doc_count(kpos, lengths))
        for h in range(heads):
            cols = slice(h * HEAD_SIZE, (h + 1) * HEAD_SIZE)
            g = (h // per) * HEAD_SIZE
            scores = lax.dot_general(
                rows_ref[:, cols], keys(g), (((1,), (1,)), ((), ())), preferred_element_type=F32
            ) * scale
            allowed = ok & (gap < windows[base + h])
            scores = jnp.where(allowed, scores, NEG_LARGE)
            now = jnp.max(scores, axis=1, keepdims=True)
            if not start:
                before = top[:, h : h + 1]
                now = jnp.maximum(now, before)
                fade = jnp.exp(before - now)
            weights = jnp.where(allowed, jnp.exp(scores - now), 0.0)
            total = jnp.sum(weights, axis=1, keepdims=True)
            product = jnp.dot(weights.astype(BF16), values(g), preferred_element_type=F32)
            top[:, h : h + 1] = now
            if start:
                den[:, h : h + 1] = total
                acc[:, cols] = product
            else:
                den[:, h : h + 1] = den[:, h : h + 1] * fade + total
                acc[:, cols] = acc[:, cols] * fade + product

    kw = shared * HEAD_SIZE
    piece(
        0,
        lambda g: rows_ref[:, qw + g : qw + g + HEAD_SIZE],
        lambda g: rows_ref[:, qw + kw + g : qw + kw + g + HEAD_SIZE],
        True,
    )
    first_doc = doc_scalar(first, lengths)

    def turn(d, carry):
        end = first - (d - 1) * tokens - 1
        touches = (end >= 0) & (first - end < widest) & (doc_scalar(end, lengths) == first_doc)

        @pl.when(touches)
        def _():
            piece(
                d,
                lambda g: kv_ref[d - 1, :, g : g + HEAD_SIZE],
                lambda g: kv_ref[d - 1, :, kw + g : kw + g + HEAD_SIZE],
                False,
            )

        return carry

    lax.fori_loop(1, kv_ref.shape[0] + 1, turn, 0)
    for h in range(heads):
        cols = slice(h * HEAD_SIZE, (h + 1) * HEAD_SIZE)
        result = (acc[:, cols] / den[:, h : h + 1]).astype(BF16)
        sum_ref[:, cols] = jnp.sum(result.astype(F32), axis=0, keepdims=True)
        full[:, cols] = result
    split_tokens(ids, full, own_ref, other_ref, half)


SMEM = pl.BlockSpec(memory_space=pltpu.SMEM)
VMEM = pl.BlockSpec(memory_space=pltpu.VMEM)


def call(kernel, scalars, arrays, outs, scratch=(), name=None):
    return pl.pallas_call(
        kernel,
        out_shape=[jax.ShapeDtypeStruct(shape, dtype) for shape, dtype in outs],
        in_specs=[SMEM] * len(scalars) + [VMEM] * len(arrays),
        out_specs=[VMEM] * len(outs),
        scratch_shapes=list(scratch),
        name=name,
    )(*scalars, *arrays)


def pack(parts, tensor):
    rows = parts[0].shape[0]
    split = [p.reshape(rows, tensor, PAIR, p.shape[1] // (tensor * PAIR)) for p in parts]
    joined = jnp.concatenate(split, axis=3)
    return joined.transpose(2, 1, 0, 3).reshape(PAIR * tensor, rows, joined.shape[3])


def to_heads(parts, tensor):
    packed = pack(parts, tensor)
    moved = lax.all_to_all(packed, ("core", "tensor"), split_axis=0, concat_axis=0, tiled=True)
    return moved.reshape(moved.shape[0] * moved.shape[1], moved.shape[2])


def earlier(block, chips):
    return [
        lax.ppermute(block, "chip", [(i, i + d) for i in range(chips - d)])
        for d in range(1, chips)
    ]


def half_columns(x, core):
    width = x.shape[-1] // PAIR
    return lax.dynamic_slice_in_dim(x, core * width, width, x.ndim - 1)


def swap(x):
    return lax.ppermute(x, "core", [(0, 1), (1, 0)])


def join(core, own, received):
    return jnp.where(
        core == 0,
        jnp.concatenate([own, received], axis=1),
        jnp.concatenate([received, own], axis=1),
    )


def local(
    queries, keys, values, mamba_x, mamba_b, mamba_c, mamba_dt, conv_x, conv_b, conv_c,
    dt_bias, decay_rate, skip_gain, norm_gain, windows, doc_lengths,
):
    chips = lax.axis_size("chip")
    tensor = lax.axis_size("tensor")
    core = lax.axis_index("core")
    chip = lax.axis_index("chip")
    q_heads = queries.shape[1] // HEAD_SIZE // (tensor * PAIR)
    base = (lax.axis_index("tensor") * PAIR + core) * q_heads
    ids = jnp.stack([chip, core, base]).astype(jnp.int32)

    rows = to_heads((mamba_x, mamba_b, mamba_c, mamba_dt), tensor)
    qkv = to_heads((queries, keys, values), tensor)
    tokens = rows.shape[0]
    half = tokens // PAIR
    taps = jnp.concatenate([half_columns(c, core) for c in (conv_x, conv_b, conv_c)], axis=1)
    width = taps.shape[1]
    halo = lax.ppermute(
        rows[tokens - HALO :, :width], "chip", [(i, i + 1) for i in range(chips - 1)]
    )
    prow = half_columns(jnp.stack([dt_bias, decay_rate, skip_gain]), core)
    pcol = prow.T
    gain = half_columns(norm_gain[None, :], core)
    heads = prow.shape[1]
    xw = heads * MP

    conv, pay, cum = call(
        pre_kernel,
        (ids, doc_lengths),
        (rows, halo, taps, prow),
        (((tokens, width), BF16), ((xw + 2 * heads, MN), BF16), ((tokens, heads), F32)),
        (pltpu.VMEM((HALO + tokens, 2 * MP), F32),),
        name="pre",
    )
    kv_width = qkv.shape[1] - q_heads * HEAD_SIZE
    kv = jnp.stack(earlier(qkv[:, q_heads * HEAD_SIZE :], chips))
    pays = earlier(pay, chips)
    (intra,) = call(
        intra_kernel, (ids, doc_lengths), (rows, conv, cum, prow, pcol), (((tokens, xw), F32),),
        name="intra",
    )
    qw = q_heads * HEAD_SIZE
    a_own, a_other, a_sum = call(
        attention_kernel,
        (ids, doc_lengths, windows),
        (qkv, kv),
        (((half, qw), BF16), ((half, qw), BF16), ((1, qw), F32)),
        (
            pltpu.VMEM((tokens, qw), BF16),
            pltpu.VMEM((tokens, 128), F32),
            pltpu.VMEM((tokens, 128), F32),
            pltpu.VMEM((tokens, qw), F32),
        ),
        name="attention",
    )
    a_received = swap(a_other)
    m_own, m_other, m_sum = call(
        functools.partial(finish_kernel, chips - 1),
        (ids, doc_lengths),
        (*pays, intra, conv, cum, gain),
        (((half, xw), BF16), ((half, xw), BF16), ((1, xw), F32)),
        (pltpu.VMEM((tokens, xw), BF16),),
        name="finish",
    )
    m_received = swap(m_other)
    sums = lax.all_gather(jnp.concatenate([a_sum, m_sum], axis=1)[0], ("chip", "core"))
    sums = jnp.sum(sums.reshape(chips, PAIR, qw + xw), axis=0)
    return (
        join(core, a_own, a_received),
        join(core, m_own, m_received),
        sums[:, :qw].reshape(PAIR * qw),
        sums[:, qw:].reshape(PAIR * xw),
    )


def solution(mesh):
    seq, tensor = mesh.shape["seq"], mesh.shape["tensor"]
    paired = Mesh(mesh.devices.reshape(seq // PAIR, PAIR, tensor), ("chip", "core", "tensor"))
    tokens = ("chip", "core", "tensor")
    block = ("chip", "core")
    placed = (P(tokens, None),) * 7 + (P(None, "tensor"),) * 3 + (P("tensor"),) * 4 + (P(), P())
    return jax.shard_map(
        local,
        mesh=paired,
        in_specs=placed,
        out_specs=(P(block, "tensor"), P(block, "tensor"), P("tensor"), P("tensor")),
        check_vma=False,
    )
```

```python
import functools
import math

import jax
import jax.numpy as jnp
from jax import lax
from jax.experimental import pallas as pl
from jax.experimental.pallas import tpu as pltpu
from jax.sharding import Mesh, PartitionSpec as P

HEAD_SIZE = 128
MP = 64
MN = 128
KC = 4
HALO = 8
NEG_LARGE = -1e30
EPS_NORM = 1e-05
PAIR = 2


F32 = jnp.float32
BF16 = jnp.bfloat16


def doc_count(pos, lengths_ref):
    start = jnp.int32(0)
    count = jnp.zeros(pos.shape, jnp.int32) if not isinstance(pos, int) else jnp.int32(0)
    for k in range(lengths_ref.shape[0]):
        count = count + jnp.where(pos >= start, 1, 0)
        start = start + lengths_ref[k]
    return count


def doc_scalar(pos, lengths_ref):
    start = jnp.int32(0)
    count = jnp.int32(0)
    for k in range(lengths_ref.shape[0]):
        count = count + (pos >= start).astype(jnp.int32)
        start = start + lengths_ref[k]
    return count


def softplus(x):
    return jnp.maximum(x, 0.0) + jnp.log1p(jnp.exp(-jnp.abs(x)))


def pair_lanes(first, second, rows):
    lane = lax.broadcasted_iota(jnp.int32, (rows, 2 * MP), 1)
    return jnp.where(lane < MP, first, second)


def pre_kernel(ids, lengths, rows_ref, halo_ref, taps_ref, prow_ref, conv_ref, pay_ref, cum_ref, ext):
    tokens = rows_ref.shape[0]
    width = taps_ref.shape[1]
    heads = prow_ref.shape[1]
    xw = width - 2 * MN
    first = ids[0] * tokens
    pos = first + lax.broadcasted_iota(jnp.int32, (tokens, 1), 0)
    here = doc_count(pos, lengths)
    same = [(doc_count(pos - j, lengths) == here).astype(F32) for j in range(1, KC)]
    step = 2 * MP
    for c in range(0, width, step):
        ext[0:HALO, :] = halo_ref[:, c : c + step].astype(F32)
        ext[HALO : HALO + tokens, :] = rows_ref[:, c : c + step].astype(F32)
        taps = taps_ref[:, c : c + step].astype(F32)
        u = taps[0:1, :] * ext[HALO : HALO + tokens, :]
        for j in range(1, KC):
            u = u + (taps[j : j + 1, :] * ext[HALO - j : HALO - j + tokens, :]) * same[j - 1]
        conv_ref[:, c : c + step] = (u / (1.0 + jnp.exp(-u))).astype(BF16)
    delta = softplus(rows_ref[:, width : width + heads].astype(F32) + prow_ref[0:1, :])
    logd = -delta * prow_ref[1:2, :]
    r = lax.broadcasted_iota(jnp.int32, (tokens, tokens), 0)
    s = lax.broadcasted_iota(jnp.int32, (tokens, tokens), 1)
    cum = jnp.dot(
        (r >= s).astype(F32), logd, precision=lax.Precision.HIGHEST, preferred_element_type=F32
    )
    cum_ref[...] = cum
    last_doc = doc_scalar(first + tokens - 1, lengths)
    to_end = jnp.where(here == last_doc, jnp.exp(cum[tokens - 1 : tokens, :] - cum), 0.0) * delta
    bc = conv_ref[:, xw : xw + MN]
    for k in range(heads // 2):
        weighted = (
            conv_ref[:, k * step : (k + 1) * step].astype(F32)
            * pair_lanes(to_end[:, 2 * k : 2 * k + 1], to_end[:, 2 * k + 1 : 2 * k + 2], tokens)
        ).astype(BF16)
        state = lax.dot_general(
            weighted, bc, (((0,), (0,)), ((), ())), preferred_element_type=F32
        )
        pay_ref[k * step : (k + 1) * step, :] = state.astype(BF16)
    ones = jnp.ones((tokens, MN), F32)
    total = lax.dot_general(
        logd, ones, (((0,), (0,)), ((), ())), precision=lax.Precision.HIGHEST,
        preferred_element_type=F32,
    )
    high = total.astype(BF16)
    pay_ref[xw : xw + heads, :] = high
    pay_ref[xw + heads : xw + 2 * heads, :] = (total - high.astype(F32)).astype(BF16)


def intra_kernel(ids, lengths, rows_ref, conv_ref, cum_ref, prow_ref, pcol_ref, out_ref):
    tokens = rows_ref.shape[0]
    heads = prow_ref.shape[1]
    xw = heads * MP
    half = tokens // PAIR
    step = 2 * MP
    dt = rows_ref[:, xw + 2 * MN : xw + 2 * MN + heads]
    eye = (
        lax.broadcasted_iota(jnp.int32, (heads, heads), 0)
        == lax.broadcasted_iota(jnp.int32, (heads, heads), 1)
    ).astype(BF16)
    dt_t = lax.dot_general(eye, dt, (((1,), (1,)), ((), ())), preferred_element_type=F32)
    delta_t = softplus(dt_t + pcol_ref[:, 0:1])
    logd_t = -delta_t * pcol_ref[:, 1:2]
    r = lax.broadcasted_iota(jnp.int32, (tokens, tokens), 0)
    s = lax.broadcasted_iota(jnp.int32, (tokens, tokens), 1)
    cum_t = jnp.dot(
        logd_t, (r <= s).astype(F32), precision=lax.Precision.HIGHEST, preferred_element_type=F32
    )
    first = ids[0] * tokens
    for b in range(PAIR):
        top, end = b * half, (b + 1) * half
        rpos = first + top + lax.broadcasted_iota(jnp.int32, (half, 1), 0)
        cpos = first + lax.broadcasted_iota(jnp.int32, (1, end), 1)
        allowed = (rpos >= cpos) & (doc_count(rpos, lengths) == doc_count(cpos, lengths))
        cross = lax.dot_general(
            conv_ref[top:end, xw + MN : xw + 2 * MN],
            conv_ref[0:end, xw : xw + MN],
            (((1,), (1,)), ((), ())),
            preferred_element_type=F32,
        )
        cross = jnp.where(allowed, cross, 0.0)
        lane = lax.broadcasted_iota(jnp.int32, (half, step), 1)
        for k in range(heads // 2):
            inputs = conv_ref[0:end, k * step : (k + 1) * step]
            parts = []
            for h in (2 * k, 2 * k + 1):
                gaps = cum_ref[top:end, h : h + 1] - cum_t[h : h + 1, 0:end]
                mix = cross * jnp.exp(jnp.minimum(gaps, 0.0)) * delta_t[h : h + 1, 0:end]
                parts.append(jnp.dot(mix.astype(BF16), inputs, preferred_element_type=F32))
            skip = jnp.where(
                lane < MP, prow_ref[2:3, 2 * k : 2 * k + 1], prow_ref[2:3, 2 * k + 1 : 2 * k + 2]
            )
            own = conv_ref[top:end, k * step : (k + 1) * step].astype(F32)
            out_ref[top:end, k * step : (k + 1) * step] = (
                jnp.where(lane < MP, parts[0], parts[1]) + skip * own
            )


def finish_kernel(count, ids, lengths, *refs):
    pays = refs[:count]
    intra_ref, conv_ref, cum_ref, gain_ref, own_ref, other_ref, sum_ref, full = refs[count:]
    tokens = intra_ref.shape[0]
    heads = cum_ref.shape[1]
    xw = heads * MP
    step = 2 * MP
    half = tokens // PAIR
    first = ids[0] * tokens
    incoming = jnp.zeros((heads, MP, MN), F32)
    total = jnp.zeros((heads, MN), F32)
    prior_doc = doc_scalar(first - 1, lengths)
    for d in range(1, count + 1):
        pay = pays[d - 1]
        reached = (doc_scalar(first - (d - 1) * tokens - 1, lengths) == prior_doc).astype(F32)
        weight = jnp.exp(total) * reached
        incoming = incoming + pay[0:xw, :].astype(F32).reshape(heads, MP, MN) * weight[:, None, :]
        total = (
            total
            + pay[xw : xw + heads, :].astype(F32)
            + pay[xw + heads : xw + 2 * heads, :].astype(F32)
        )
    state = incoming.reshape(xw, MN).astype(BF16)
    pos = first + lax.broadcasted_iota(jnp.int32, (tokens, 1), 0)
    inflow = jnp.where(doc_count(pos, lengths) == prior_doc, jnp.exp(cum_ref[...]), 0.0)
    cc = conv_ref[:, xw + MN : xw + 2 * MN]
    same_head = (
        lax.broadcasted_iota(jnp.int32, (step, step), 0) // MP
        == lax.broadcasted_iota(jnp.int32, (step, step), 1) // MP
    )
    mean = jnp.where(same_head, 1.0 / MP, 0.0).astype(BF16)
    for k in range(heads // 2):
        cols = slice(k * step, (k + 1) * step)
        entering = lax.dot_general(
            cc, state[cols, :], (((1,), (1,)), ((), ())), preferred_element_type=F32
        )
        mixed = intra_ref[:, cols] + entering * pair_lanes(
            inflow[:, 2 * k : 2 * k + 1], inflow[:, 2 * k + 1 : 2 * k + 2], tokens
        )
        square = mixed * mixed
        high = square.astype(BF16)
        low = (square - high.astype(F32)).astype(BF16)
        mean_square = jnp.dot(high, mean, preferred_element_type=F32) + jnp.dot(
            low, mean, preferred_element_type=F32
        )
        normed = (mixed * lax.rsqrt(mean_square + EPS_NORM) * gain_ref[0:1, cols]).astype(BF16)
        sum_ref[:, cols] = jnp.sum(normed.astype(F32), axis=0, keepdims=True)
        full[:, cols] = normed
    split_tokens(ids, full, own_ref, other_ref, half)


def split_tokens(ids, full, own_ref, other_ref, half):
    @pl.when(ids[1] == 0)
    def _():
        own_ref[...] = full[0:half, :]
        other_ref[...] = full[half:, :]

    @pl.when(ids[1] != 0)
    def _():
        own_ref[...] = full[half:, :]
        other_ref[...] = full[0:half, :]


def attention_kernel(
    ids, lengths, windows, rows_ref, here_ref, kv_ref, own_ref, other_ref, sum_ref, full, top, den, acc
):
    tokens = rows_ref.shape[0]
    shared = kv_ref.shape[2] // (2 * HEAD_SIZE)
    heads = full.shape[1] // HEAD_SIZE
    per = heads // shared
    half = tokens // PAIR
    first = ids[0] * tokens
    base = ids[2]
    widest = windows[base]
    for h in range(1, heads):
        widest = jnp.maximum(widest, windows[base + h])
    qpos = first + lax.broadcasted_iota(jnp.int32, (tokens, 1), 0)
    qdoc = doc_count(qpos, lengths)
    scale = 1.0 / math.sqrt(HEAD_SIZE)

    def piece(d, keys, values, start):
        kpos = (first - d * tokens) + lax.broadcasted_iota(jnp.int32, (1, tokens), 1)
        gap = qpos - kpos
        ok = (gap >= 0) & (kpos >= 0) & (qdoc == doc_count(kpos, lengths))
        for h in range(heads):
            cols = slice(h * HEAD_SIZE, (h + 1) * HEAD_SIZE)
            g = (h // per) * HEAD_SIZE
            scores = lax.dot_general(
                rows_ref[:, cols], keys(g), (((1,), (1,)), ((), ())), preferred_element_type=F32
            ) * scale
            allowed = ok & (gap < windows[base + h])
            scores = jnp.where(allowed, scores, NEG_LARGE)
            now = jnp.max(scores, axis=1, keepdims=True)
            if not start:
                before = top[:, h : h + 1]
                now = jnp.maximum(now, before)
                fade = jnp.exp(before - now)
            weights = jnp.where(allowed, jnp.exp(scores - now), 0.0)
            total = jnp.sum(weights, axis=1, keepdims=True)
            product = jnp.dot(weights.astype(BF16), values(g), preferred_element_type=F32)
            top[:, h : h + 1] = now
            if start:
                den[:, h : h + 1] = total
                acc[:, cols] = product
            else:
                den[:, h : h + 1] = den[:, h : h + 1] * fade + total
                acc[:, cols] = acc[:, cols] * fade + product

    kw = shared * HEAD_SIZE
    piece(
        0,
        lambda g: here_ref[:, g : g + HEAD_SIZE],
        lambda g: here_ref[:, kw + g : kw + g + HEAD_SIZE],
        True,
    )
    first_doc = doc_scalar(first, lengths)

    def turn(d, carry):
        end = first - (d - 1) * tokens - 1
        touches = (end >= 0) & (first - end < widest) & (doc_scalar(end, lengths) == first_doc)

        @pl.when(touches)
        def _():
            piece(
                d,
                lambda g: kv_ref[d - 1, :, g : g + HEAD_SIZE],
                lambda g: kv_ref[d - 1, :, kw + g : kw + g + HEAD_SIZE],
                False,
            )

        return carry

    lax.fori_loop(1, kv_ref.shape[0] + 1, turn, 0)
    for h in range(heads):
        cols = slice(h * HEAD_SIZE, (h + 1) * HEAD_SIZE)
        result = (acc[:, cols] / den[:, h : h + 1]).astype(BF16)
        sum_ref[:, cols] = jnp.sum(result.astype(F32), axis=0, keepdims=True)
        full[:, cols] = result
    split_tokens(ids, full, own_ref, other_ref, half)


SMEM = pl.BlockSpec(memory_space=pltpu.SMEM)
VMEM = pl.BlockSpec(memory_space=pltpu.VMEM)


def call(kernel, scalars, arrays, outs, scratch=(), name=None):
    return pl.pallas_call(
        kernel,
        out_shape=[jax.ShapeDtypeStruct(shape, dtype) for shape, dtype in outs],
        in_specs=[SMEM] * len(scalars) + [VMEM] * len(arrays),
        out_specs=[VMEM] * len(outs),
        scratch_shapes=list(scratch),
        name=name,
    )(*scalars, *arrays)


def pack_kernel(*refs):
    out_ref = refs[-1]
    tensor = out_ref.shape[0] // PAIR
    for core in range(PAIR):
        for t in range(tensor):
            col = 0
            for part in refs[:-1]:
                width = part.shape[1] // (tensor * PAIR)
                at = (t * PAIR + core) * width
                out_ref[core * tensor + t, :, col : col + width] = part[:, at : at + width]
                col += width


def pack(parts, tensor):
    ways = PAIR * tensor
    shape = (ways, parts[0].shape[0], sum(p.shape[1] for p in parts) // ways)
    return call(pack_kernel, (), parts, ((shape, BF16),), name="pack")[0]


def to_heads(packed):
    moved = lax.all_to_all(packed, ("core", "tensor"), split_axis=0, concat_axis=0, tiled=True)
    return moved.reshape(moved.shape[0] * moved.shape[1], moved.shape[2])


def join_kernel(ids, own_ref, received_ref, out_ref):
    width = own_ref.shape[1]

    @pl.when(ids[1] == 0)
    def _():
        out_ref[:, :width] = own_ref[...]
        out_ref[:, width:] = received_ref[...]

    @pl.when(ids[1] != 0)
    def _():
        out_ref[:, :width] = received_ref[...]
        out_ref[:, width:] = own_ref[...]


def join_tokens(ids, own, received):
    shape = (own.shape[0], PAIR * own.shape[1])
    return call(join_kernel, (ids,), (own, received), ((shape, BF16),), name="join")[0]


def sum_over_chips(x, chips):
    if chips & (chips - 1):
        return lax.psum(x, "chip")
    bit = 1
    while bit < chips:
        x = x + lax.ppermute(x, "chip", [(i, i ^ bit) for i in range(chips)])
        bit *= 2
    return x


def earlier(block, chips):
    return [
        lax.ppermute(block, "chip", [(i, i + d) for i in range(chips - d)])
        for d in range(1, chips)
    ]


def half_columns(x, core):
    width = x.shape[-1] // PAIR
    return lax.dynamic_slice_in_dim(x, core * width, width, x.ndim - 1)


def swap(x):
    return lax.ppermute(x, "core", [(0, 1), (1, 0)])


def join(core, own, received):
    return jnp.where(
        core == 0,
        jnp.concatenate([own, received], axis=1),
        jnp.concatenate([received, own], axis=1),
    )


def local(
    queries, keys, values, mamba_x, mamba_b, mamba_c, mamba_dt, conv_x, conv_b, conv_c,
    dt_bias, decay_rate, skip_gain, norm_gain, windows, doc_lengths,
):
    chips = lax.axis_size("chip")
    tensor = lax.axis_size("tensor")
    core = lax.axis_index("core")
    chip = lax.axis_index("chip")
    q_heads = queries.shape[1] // HEAD_SIZE // (tensor * PAIR)
    base = (lax.axis_index("tensor") * PAIR + core) * q_heads
    ids = jnp.stack([chip, core, base]).astype(jnp.int32)

    here_kv = to_heads(pack((keys, values), tensor))
    packed, here_kv = lax.optimization_barrier(
        (pack((mamba_x, mamba_b, mamba_c, mamba_dt), tensor), here_kv)
    )
    rows = to_heads(packed)
    packed, rows, pieces = lax.optimization_barrier(
        (pack((queries,), tensor), rows, earlier(here_kv, chips))
    )
    query_rows = to_heads(packed)
    tokens = rows.shape[0]
    half = tokens // PAIR
    taps = jnp.concatenate([half_columns(c, core) for c in (conv_x, conv_b, conv_c)], axis=1)
    width = taps.shape[1]
    halo = lax.ppermute(
        rows[tokens - HALO :, :width], "chip", [(i, i + 1) for i in range(chips - 1)]
    )
    prow = half_columns(jnp.stack([dt_bias, decay_rate, skip_gain]), core)
    pcol = prow.T
    gain = half_columns(norm_gain[None, :], core)
    heads = prow.shape[1]
    xw = heads * MP

    conv, pay, cum = call(
        pre_kernel,
        (ids, doc_lengths),
        (rows, halo, taps, prow),
        (((tokens, width), BF16), ((xw + 2 * heads, MN), BF16), ((tokens, heads), F32)),
        (pltpu.VMEM((HALO + tokens, 2 * MP), F32),),
        name="pre",
    )
    kv = jnp.stack(pieces)
    pays = earlier(pay, chips)
    (intra,) = call(
        intra_kernel, (ids, doc_lengths), (rows, conv, cum, prow, pcol), (((tokens, xw), F32),),
        name="intra",
    )
    qw = q_heads * HEAD_SIZE
    a_own, a_other, a_sum = call(
        attention_kernel,
        (ids, doc_lengths, windows),
        (query_rows, here_kv, kv),
        (((half, qw), BF16), ((half, qw), BF16), ((1, qw), F32)),
        (
            pltpu.VMEM((tokens, qw), BF16),
            pltpu.VMEM((tokens, 128), F32),
            pltpu.VMEM((tokens, 128), F32),
            pltpu.VMEM((tokens, qw), F32),
        ),
        name="attention",
    )
    attn = join_tokens(ids, a_own, swap(a_other))
    intra, attn, a_sum = lax.optimization_barrier((intra, attn, a_sum))
    m_own, m_other, m_sum = call(
        functools.partial(finish_kernel, chips - 1),
        (ids, doc_lengths),
        (*pays, intra, conv, cum, gain),
        (((half, xw), BF16), ((half, xw), BF16), ((1, xw), F32)),
        (pltpu.VMEM((tokens, xw), BF16),),
        name="finish",
    )
    m_received = swap(m_other)
    sums = sum_over_chips(jnp.concatenate([a_sum, m_sum], axis=1), chips)
    sums_received = swap(sums)
    return (
        attn,
        join_tokens(ids, m_own, m_received),
        join(core, sums[:, :qw], sums_received[:, :qw])[0],
        join(core, sums[:, qw:], sums_received[:, qw:])[0],
    )


def solution(mesh):
    seq, tensor = mesh.shape["seq"], mesh.shape["tensor"]
    paired = Mesh(mesh.devices.reshape(seq // PAIR, PAIR, tensor), ("chip", "core", "tensor"))
    tokens = ("chip", "core", "tensor")
    block = ("chip", "core")
    placed = (P(tokens, None),) * 7 + (P(None, "tensor"),) * 3 + (P("tensor"),) * 4 + (P(), P())
    return jax.shard_map(
        local,
        mesh=paired,
        in_specs=placed,
        out_specs=(P(block, "tensor"), P(block, "tensor"), P("tensor"), P("tensor")),
        check_vma=False,
    )
```

```python
import math

import jax
import jax.numpy as jnp
from jax import lax
from jax.experimental import pallas as pl
from jax.experimental.pallas import tpu as pltpu
from jax.sharding import Mesh, PartitionSpec as P

HEAD_SIZE = 128
MP = 64
MN = 128
KC = 4
HALO = 8
NEG_LARGE = -1e30
EPS_NORM = 1e-05
PAIR = 2


F32 = jnp.float32
BF16 = jnp.bfloat16


def doc_count(pos, lengths_ref):
    start = jnp.int32(0)
    count = jnp.zeros(pos.shape, jnp.int32) if not isinstance(pos, int) else jnp.int32(0)
    for k in range(lengths_ref.shape[0]):
        count = count + jnp.where(pos >= start, 1, 0)
        start = start + lengths_ref[k]
    return count


def doc_scalar(pos, lengths_ref):
    start = jnp.int32(0)
    count = jnp.int32(0)
    for k in range(lengths_ref.shape[0]):
        count = count + (pos >= start).astype(jnp.int32)
        start = start + lengths_ref[k]
    return count


def softplus(x):
    return jnp.maximum(x, 0.0) + jnp.log1p(jnp.exp(-jnp.abs(x)))


def pair_lanes(first, second, rows):
    lane = lax.broadcasted_iota(jnp.int32, (rows, 2 * MP), 1)
    return jnp.where(lane < MP, first, second)


def pre_kernel(ids, lengths, rows_ref, halo_ref, taps_ref, prow_ref, conv_ref, pay_ref, cum_ref, ext):
    tokens = rows_ref.shape[0]
    width = taps_ref.shape[1]
    heads = prow_ref.shape[1]
    xw = width - 2 * MN
    first = ids[0] * tokens
    pos = first + lax.broadcasted_iota(jnp.int32, (tokens, 1), 0)
    here = doc_count(pos, lengths)
    same = [(doc_count(pos - j, lengths) == here).astype(F32) for j in range(1, KC)]
    step = 2 * MP
    for c in range(0, width, step):
        ext[0:HALO, :] = halo_ref[:, c : c + step].astype(F32)
        ext[HALO : HALO + tokens, :] = rows_ref[:, c : c + step].astype(F32)
        taps = taps_ref[:, c : c + step].astype(F32)
        u = taps[0:1, :] * ext[HALO : HALO + tokens, :]
        for j in range(1, KC):
            u = u + (taps[j : j + 1, :] * ext[HALO - j : HALO - j + tokens, :]) * same[j - 1]
        conv_ref[:, c : c + step] = (u / (1.0 + jnp.exp(-u))).astype(BF16)
    delta = softplus(rows_ref[:, width : width + heads].astype(F32) + prow_ref[0:1, :])
    logd = -delta * prow_ref[1:2, :]
    r = lax.broadcasted_iota(jnp.int32, (tokens, tokens), 0)
    s = lax.broadcasted_iota(jnp.int32, (tokens, tokens), 1)
    cum = jnp.dot(
        (r >= s).astype(F32), logd, precision=lax.Precision.HIGHEST, preferred_element_type=F32
    )
    cum_ref[...] = cum
    last_doc = doc_scalar(first + tokens - 1, lengths)
    to_end = jnp.where(here == last_doc, jnp.exp(cum[tokens - 1 : tokens, :] - cum), 0.0) * delta
    bc = conv_ref[:, xw : xw + MN]
    for k in range(heads // 2):
        weighted = (
            conv_ref[:, k * step : (k + 1) * step].astype(F32)
            * pair_lanes(to_end[:, 2 * k : 2 * k + 1], to_end[:, 2 * k + 1 : 2 * k + 2], tokens)
        ).astype(BF16)
        state = lax.dot_general(
            weighted, bc, (((0,), (0,)), ((), ())), preferred_element_type=F32
        )
        for to in range(pay_ref.shape[0]):
            pay_ref[to, k * step : (k + 1) * step, :] = state.astype(BF16)
    ones = jnp.ones((tokens, MN), F32)
    total = lax.dot_general(
        logd, ones, (((0,), (0,)), ((), ())), precision=lax.Precision.HIGHEST,
        preferred_element_type=F32,
    )
    high = total.astype(BF16)
    for to in range(pay_ref.shape[0]):
        pay_ref[to, xw : xw + heads, :] = high
        pay_ref[to, xw + heads : xw + 2 * heads, :] = (total - high.astype(F32)).astype(BF16)


def intra_kernel(ids, lengths, rows_ref, conv_ref, cum_ref, prow_ref, pcol_ref, out_ref):
    tokens = rows_ref.shape[0]
    heads = prow_ref.shape[1]
    xw = heads * MP
    half = tokens // PAIR
    step = 2 * MP
    dt = rows_ref[:, xw + 2 * MN : xw + 2 * MN + heads]
    eye = (
        lax.broadcasted_iota(jnp.int32, (heads, heads), 0)
        == lax.broadcasted_iota(jnp.int32, (heads, heads), 1)
    ).astype(BF16)
    dt_t = lax.dot_general(eye, dt, (((1,), (1,)), ((), ())), preferred_element_type=F32)
    delta_t = softplus(dt_t + pcol_ref[:, 0:1])
    logd_t = -delta_t * pcol_ref[:, 1:2]
    r = lax.broadcasted_iota(jnp.int32, (tokens, tokens), 0)
    s = lax.broadcasted_iota(jnp.int32, (tokens, tokens), 1)
    cum_t = jnp.dot(
        logd_t, (r <= s).astype(F32), precision=lax.Precision.HIGHEST, preferred_element_type=F32
    )
    first = ids[0] * tokens
    for b in range(PAIR):
        top, end = b * half, (b + 1) * half
        rpos = first + top + lax.broadcasted_iota(jnp.int32, (half, 1), 0)
        cpos = first + lax.broadcasted_iota(jnp.int32, (1, end), 1)
        allowed = (rpos >= cpos) & (doc_count(rpos, lengths) == doc_count(cpos, lengths))
        cross = lax.dot_general(
            conv_ref[top:end, xw + MN : xw + 2 * MN],
            conv_ref[0:end, xw : xw + MN],
            (((1,), (1,)), ((), ())),
            preferred_element_type=F32,
        )
        cross = jnp.where(allowed, cross, 0.0)
        lane = lax.broadcasted_iota(jnp.int32, (half, step), 1)
        for k in range(heads // 2):
            inputs = conv_ref[0:end, k * step : (k + 1) * step]
            parts = []
            for h in (2 * k, 2 * k + 1):
                gaps = cum_ref[top:end, h : h + 1] - cum_t[h : h + 1, 0:end]
                mix = cross * jnp.exp(jnp.minimum(gaps, 0.0)) * delta_t[h : h + 1, 0:end]
                parts.append(jnp.dot(mix.astype(BF16), inputs, preferred_element_type=F32))
            skip = jnp.where(
                lane < MP, prow_ref[2:3, 2 * k : 2 * k + 1], prow_ref[2:3, 2 * k + 1 : 2 * k + 2]
            )
            own = conv_ref[top:end, k * step : (k + 1) * step].astype(F32)
            out_ref[top:end, k * step : (k + 1) * step] = (
                jnp.where(lane < MP, parts[0], parts[1]) + skip * own
            )


def finish_kernel(
    ids, lengths, pays_ref, intra_ref, conv_ref, cum_ref, gain_ref, attn_sum_ref,
    own_ref, other_ref, sum_ref, full,
):
    qw = attn_sum_ref.shape[1]
    tokens = intra_ref.shape[0]
    heads = cum_ref.shape[1]
    xw = heads * MP
    step = 2 * MP
    half = tokens // PAIR
    first = ids[0] * tokens
    incoming = jnp.zeros((heads, MP, MN), F32)
    total = jnp.zeros((heads, MN), F32)
    prior_doc = doc_scalar(first - 1, lengths)
    for d in range(1, pays_ref.shape[0]):
        source = ids[0] - d
        pay = pays_ref.at[jnp.maximum(source, 0)]
        end = first - (d - 1) * tokens - 1
        reached = ((source >= 0) & (doc_scalar(end, lengths) == prior_doc)).astype(F32)
        weight = jnp.exp(total) * reached
        incoming = incoming + pay[0:xw, :].astype(F32).reshape(heads, MP, MN) * weight[:, None, :]
        total = (
            total
            + pay[xw : xw + heads, :].astype(F32)
            + pay[xw + heads : xw + 2 * heads, :].astype(F32)
        )
    state = incoming.reshape(xw, MN).astype(BF16)
    pos = first + lax.broadcasted_iota(jnp.int32, (tokens, 1), 0)
    inflow = jnp.where(doc_count(pos, lengths) == prior_doc, jnp.exp(cum_ref[...]), 0.0)
    cc = conv_ref[:, xw + MN : xw + 2 * MN]
    same_head = (
        lax.broadcasted_iota(jnp.int32, (step, step), 0) // MP
        == lax.broadcasted_iota(jnp.int32, (step, step), 1) // MP
    )
    mean = jnp.where(same_head, 1.0 / MP, 0.0).astype(BF16)
    for k in range(heads // 2):
        cols = slice(k * step, (k + 1) * step)
        entering = lax.dot_general(
            cc, state[cols, :], (((1,), (1,)), ((), ())), preferred_element_type=F32
        )
        mixed = intra_ref[:, cols] + entering * pair_lanes(
            inflow[:, 2 * k : 2 * k + 1], inflow[:, 2 * k + 1 : 2 * k + 2], tokens
        )
        square = mixed * mixed
        high = square.astype(BF16)
        low = (square - high.astype(F32)).astype(BF16)
        mean_square = jnp.dot(high, mean, preferred_element_type=F32) + jnp.dot(
            low, mean, preferred_element_type=F32
        )
        normed = (mixed * lax.rsqrt(mean_square + EPS_NORM) * gain_ref[0:1, cols]).astype(BF16)
        column = jnp.sum(normed.astype(F32), axis=0, keepdims=True)
        sum_ref[:, :, qw + k * step : qw + (k + 1) * step] = jnp.broadcast_to(
            column[None], (sum_ref.shape[0], 1, step)
        )
        full[:, cols] = normed
    sum_ref[:, :, :qw] = jnp.broadcast_to(
        attn_sum_ref[...][None], (sum_ref.shape[0], 1, qw)
    )
    split_tokens(ids, full, own_ref, other_ref, half)


def split_tokens(ids, full, own_ref, other_ref, half):
    @pl.when(ids[1] == 0)
    def _():
        own_ref[...] = full[0:half, :]
        other_ref[...] = full[half:, :]

    @pl.when(ids[1] != 0)
    def _():
        own_ref[...] = full[half:, :]
        other_ref[...] = full[0:half, :]


def attention_kernel(
    ids, lengths, windows, rows_ref, here_ref, kv_ref, own_ref, other_ref, sum_ref, full, top, den, acc
):
    tokens = rows_ref.shape[0]
    shared = kv_ref.shape[2] // (2 * HEAD_SIZE)
    heads = full.shape[1] // HEAD_SIZE
    per = heads // shared
    half = tokens // PAIR
    first = ids[0] * tokens
    base = ids[2]
    widest = windows[base]
    for h in range(1, heads):
        widest = jnp.maximum(widest, windows[base + h])
    qpos = first + lax.broadcasted_iota(jnp.int32, (tokens, 1), 0)
    qdoc = doc_count(qpos, lengths)
    scale = 1.0 / math.sqrt(HEAD_SIZE)

    def piece(d, keys, values, start):
        kpos = (first - d * tokens) + lax.broadcasted_iota(jnp.int32, (1, tokens), 1)
        gap = qpos - kpos
        ok = (gap >= 0) & (kpos >= 0) & (qdoc == doc_count(kpos, lengths))
        for h in range(heads):
            cols = slice(h * HEAD_SIZE, (h + 1) * HEAD_SIZE)
            g = (h // per) * HEAD_SIZE
            scores = lax.dot_general(
                rows_ref[:, cols], keys(g), (((1,), (1,)), ((), ())), preferred_element_type=F32
            ) * scale
            allowed = ok & (gap < windows[base + h])
            scores = jnp.where(allowed, scores, NEG_LARGE)
            now = jnp.max(scores, axis=1, keepdims=True)
            if not start:
                before = top[:, h : h + 1]
                now = jnp.maximum(now, before)
                fade = jnp.exp(before - now)
            weights = jnp.where(allowed, jnp.exp(scores - now), 0.0)
            total = jnp.sum(weights, axis=1, keepdims=True)
            product = jnp.dot(weights.astype(BF16), values(g), preferred_element_type=F32)
            top[:, h : h + 1] = now
            if start:
                den[:, h : h + 1] = total
                acc[:, cols] = product
            else:
                den[:, h : h + 1] = den[:, h : h + 1] * fade + total
                acc[:, cols] = acc[:, cols] * fade + product

    kw = shared * HEAD_SIZE
    piece(
        0,
        lambda g: here_ref[:, g : g + HEAD_SIZE],
        lambda g: here_ref[:, kw + g : kw + g + HEAD_SIZE],
        True,
    )
    first_doc = doc_scalar(first, lengths)

    def turn(d, carry):
        end = first - (d - 1) * tokens - 1
        touches = (end >= 0) & (first - end < widest) & (doc_scalar(end, lengths) == first_doc)

        @pl.when(touches)
        def _():
            piece(
                d,
                lambda g: kv_ref[d - 1, :, g : g + HEAD_SIZE],
                lambda g: kv_ref[d - 1, :, kw + g : kw + g + HEAD_SIZE],
                False,
            )

        return carry

    lax.fori_loop(1, kv_ref.shape[0] + 1, turn, 0)
    for h in range(heads):
        cols = slice(h * HEAD_SIZE, (h + 1) * HEAD_SIZE)
        result = (acc[:, cols] / den[:, h : h + 1]).astype(BF16)
        sum_ref[:, cols] = jnp.sum(result.astype(F32), axis=0, keepdims=True)
        full[:, cols] = result
    split_tokens(ids, full, own_ref, other_ref, half)


SMEM = pl.BlockSpec(memory_space=pltpu.SMEM)
VMEM = pl.BlockSpec(memory_space=pltpu.VMEM)


def call(kernel, scalars, arrays, outs, scratch=(), name=None):
    return pl.pallas_call(
        kernel,
        out_shape=[jax.ShapeDtypeStruct(shape, dtype) for shape, dtype in outs],
        in_specs=[SMEM] * len(scalars) + [VMEM] * len(arrays),
        out_specs=[VMEM] * len(outs),
        scratch_shapes=list(scratch),
        name=name,
    )(*scalars, *arrays)


def pack_kernel(*refs):
    out_ref = refs[-1]
    tensor = out_ref.shape[0] // PAIR
    for core in range(PAIR):
        for t in range(tensor):
            col = 0
            for part in refs[:-1]:
                width = part.shape[1] // (tensor * PAIR)
                at = (t * PAIR + core) * width
                out_ref[core * tensor + t, :, col : col + width] = part[:, at : at + width]
                col += width


def pack(parts, tensor):
    ways = PAIR * tensor
    shape = (ways, parts[0].shape[0], sum(p.shape[1] for p in parts) // ways)
    return call(pack_kernel, (), parts, ((shape, BF16),), name="pack")[0]


def to_heads(packed):
    moved = lax.all_to_all(packed, ("core", "tensor"), split_axis=0, concat_axis=0, tiled=True)
    return moved.reshape(moved.shape[0] * moved.shape[1], moved.shape[2])


def join_kernel(ids, own_ref, received_ref, out_ref):
    width = own_ref.shape[1]

    @pl.when(ids[1] == 0)
    def _():
        out_ref[:, :width] = own_ref[...]
        out_ref[:, width:] = received_ref[...]

    @pl.when(ids[1] != 0)
    def _():
        out_ref[:, :width] = received_ref[...]
        out_ref[:, width:] = own_ref[...]


def join_tokens(ids, own, received):
    shape = (own.shape[0], PAIR * own.shape[1])
    return call(join_kernel, (ids,), (own, received), ((shape, BF16),), name="join")[0]


def sums_kernel(parts_ref, attn_ref, mamba_ref):
    qw = attn_ref.shape[1] // PAIR
    xw = mamba_ref.shape[1] // PAIR
    for core in range(PAIR):
        total = parts_ref[core]
        for k in range(core + PAIR, parts_ref.shape[0], PAIR):
            total = total + parts_ref[k]
        attn_ref[:, core * qw : (core + 1) * qw] = total[:, :qw]
        mamba_ref[:, core * xw : (core + 1) * xw] = total[:, qw:]


def earlier(block, chips):
    return [
        lax.ppermute(block, "chip", [(i, i + d) for i in range(chips - d)])
        for d in range(1, chips)
    ]


def half_columns(x, core):
    width = x.shape[-1] // PAIR
    return lax.dynamic_slice_in_dim(x, core * width, width, x.ndim - 1)


def swap(x):
    return lax.ppermute(x, "core", [(0, 1), (1, 0)])


def local(
    queries, keys, values, mamba_x, mamba_b, mamba_c, mamba_dt, conv_x, conv_b, conv_c,
    dt_bias, decay_rate, skip_gain, norm_gain, windows, doc_lengths,
):
    chips = lax.axis_size("chip")
    tensor = lax.axis_size("tensor")
    core = lax.axis_index("core")
    chip = lax.axis_index("chip")
    q_heads = queries.shape[1] // HEAD_SIZE // (tensor * PAIR)
    base = (lax.axis_index("tensor") * PAIR + core) * q_heads
    ids = jnp.stack([chip, core, base]).astype(jnp.int32)

    here_kv = to_heads(pack((keys, values), tensor))
    packed, here_kv = lax.optimization_barrier(
        (pack((mamba_x, mamba_b, mamba_c, mamba_dt), tensor), here_kv)
    )
    rows = to_heads(packed)
    rows, pieces = lax.optimization_barrier((rows, earlier(here_kv, chips)))
    tokens = rows.shape[0]
    half = tokens // PAIR
    taps = jnp.concatenate([half_columns(c, core) for c in (conv_x, conv_b, conv_c)], axis=1)
    width = taps.shape[1]
    halo = lax.ppermute(
        rows[tokens - HALO :, :width], "chip", [(i, i + 1) for i in range(chips - 1)]
    )
    query_rows = to_heads(lax.optimization_barrier((pack((queries,), tensor), rows))[0])
    prow = half_columns(jnp.stack([dt_bias, decay_rate, skip_gain]), core)
    pcol = prow.T
    gain = half_columns(norm_gain[None, :], core)
    heads = prow.shape[1]
    xw = heads * MP

    conv, pay, cum = call(
        pre_kernel,
        (ids, doc_lengths),
        (rows, halo, taps, prow),
        (((tokens, width), BF16), ((chips, xw + 2 * heads, MN), BF16), ((tokens, heads), F32)),
        (pltpu.VMEM((HALO + tokens, 2 * MP), F32),),
        name="pre",
    )
    kv = jnp.stack(pieces)
    pays = lax.all_to_all(pay, "chip", split_axis=0, concat_axis=0, tiled=True)
    (intra,) = call(
        intra_kernel, (ids, doc_lengths), (rows, conv, cum, prow, pcol), (((tokens, xw), F32),),
        name="intra",
    )
    qw = q_heads * HEAD_SIZE
    a_own, a_other, a_sum = call(
        attention_kernel,
        (ids, doc_lengths, windows),
        (query_rows, here_kv, kv),
        (((half, qw), BF16), ((half, qw), BF16), ((1, qw), F32)),
        (
            pltpu.VMEM((tokens, qw), BF16),
            pltpu.VMEM((tokens, 128), F32),
            pltpu.VMEM((tokens, 128), F32),
            pltpu.VMEM((tokens, qw), F32),
        ),
        name="attention",
    )
    a_received = swap(a_other)
    intra, a_sum, a_received = lax.optimization_barrier((intra, a_sum, a_received))
    m_own, m_other, sums = call(
        finish_kernel,
        (ids, doc_lengths),
        (pays, intra, conv, cum, gain, a_sum),
        (((half, xw), BF16), ((half, xw), BF16), ((chips * PAIR, 1, qw + xw), F32)),
        (pltpu.VMEM((tokens, xw), BF16),),
        name="finish",
    )
    m_received = swap(m_other)
    parts = lax.all_to_all(sums, ("chip", "core"), split_axis=0, concat_axis=0, tiled=True)
    attn_sum, mamba_sum = call(
        sums_kernel, (), (parts,), (((1, PAIR * qw), F32), ((1, PAIR * xw), F32)), name="sums"
    )
    return (
        join_tokens(ids, a_own, a_received),
        join_tokens(ids, m_own, m_received),
        attn_sum[0],
        mamba_sum[0],
    )


def solution(mesh):
    seq, tensor = mesh.shape["seq"], mesh.shape["tensor"]
    paired = Mesh(mesh.devices.reshape(seq // PAIR, PAIR, tensor), ("chip", "core", "tensor"))
    tokens = ("chip", "core", "tensor")
    block = ("chip", "core")
    placed = (P(tokens, None),) * 7 + (P(None, "tensor"),) * 3 + (P("tensor"),) * 4 + (P(), P())
    return jax.shard_map(
        local,
        mesh=paired,
        in_specs=placed,
        out_specs=(P(block, "tensor"), P(block, "tensor"), P("tensor"), P("tensor")),
        check_vma=False,
    )
```
